256 devices in a mesh: ep: 16 (over x, y), dp: 16 (over z, core).
Axes of the slice: x: 4, y: 4, z: 8, core: 2. Of those that a mesh axis runs over, the one named last changes fastest.
Arguments:
- tokens: float32 [32768, 1024], P(('ep', 'dp')), may hold values from -6 to 6
- cotangent: float32 [32768, 1024], P(('ep', 'dp')), may hold values from -6 to 6
- w_gate: float32 [256, 1024, 256], P(('ep', 'dp')), may hold values from -0.1875 to 0.1875
- w_up: float32 [256, 1024, 256], P(('ep', 'dp')), may hold values from -0.1875 to 0.1875
- w_down: float32 [256, 256, 1024], P(('ep', 'dp')), may hold values from -0.25 to 0.25
- expert_ids: int32 [32768, 2], P(('ep', 'dp')), may hold values from 0 to 127, as said below
- route_weight: float32 [32768, 2], P(('ep', 'dp')), may hold values from 0.25 to 1
- halted: int32 [32768], P(('ep', 'dp')), may hold values 0 or 1
Outputs:
- grad_x: float32 [32768, 1024], P(('ep', 'dp'))
- grad_gate: float32 [256, 1024, 256], P(('ep', 'dp'))
- grad_up: float32 [256, 1024, 256], P(('ep', 'dp'))
- grad_down: float32 [256, 256, 1024], P(('ep', 'dp'))
The draws below stay inside these ranges and needn't reach their ends.
Inputs may be any that keep to these rules, and one draw needn't show every extreme that they name: `expert_ids`: within the rows of one device the two ids of a token differ, no expert is named more than 3 times, and every expert whose number is a multiple of 8 is named exactly 3 times.
All inputs are finite; a program needn't handle non-finite values. No bound on the sum of `halted` on one device may be relied on, other than what follows from the above.
Results may differ from the reference program's by a relative error of at most 0.0003.
Values sent between devices are 32-bit elements; how exact they have to be, the bound alone decides.
A program may use at most 128 MiB of HBM per device.

```python
import jax
import jax.numpy as jnp
from jax import lax

D = 1024
HIDDEN_SIZE = 512
TOK_DEV = 128
HALF = 256
EXP_EP = 8
EXPERTS = 128
PIECES = 256
MOST = 3
TOKENS = 32768
N_EP = 16
N_DP = 16


def draw_expert_ids(key, part):
    block_count = TOKENS // TOK_DEV
    slot_count = EXPERTS * MOST
    expert_per_slot = jnp.repeat(jnp.arange(EXPERTS, dtype=jnp.int32), MOST)
    key_favour, key_blocks = jax.random.split(key)
    preferred_boost = jax.random.randint(key_favour, (EXPERTS,), 0, 4)
    forced_choice = (jnp.arange(EXPERTS) % EXP_EP == 0).astype(jnp.int32)
    extra_reward = (preferred_boost * 512 + forced_choice * 4096)[expert_per_slot]

    def one_block(block_key):
        key_noise, key_order, key_perm, key_flip = jax.random.split(block_key, 4)
        random_jitter = jax.random.randint(key_noise, (slot_count,), 0, 512)
        ranking_order = jax.random.permutation(key_order, slot_count)
        routing_score = (extra_reward + random_jitter) * 4096 + ranking_order
        chosen = lax.top_k(routing_score, 2 * TOK_DEV)[1]
        sorted_ids = jnp.sort(expert_per_slot[chosen])
        pairs = jnp.stack([sorted_ids[:TOK_DEV], sorted_ids[TOK_DEV:]], axis=1)
        pairs = pairs[jax.random.permutation(key_perm, TOK_DEV)]
        flip = jax.random.randint(key_flip, (TOK_DEV, 1), 0, 2)
        return jnp.where(flip == 1, pairs[:, ::-1], pairs)
    block_keys = jax.random.split(key_blocks, block_count)
    return jax.vmap(one_block)(block_keys).reshape(TOKENS, 2).astype(jnp.int32)


def with_ends(array, key, smallest, largest):
    shape = array.shape
    place = [jax.random.randint(jax.random.fold_in(key, axis), (), 0, shape[axis]) for axis in range(len(shape))]
    array = array.at[tuple(place)].set(smallest)
    longest = shape.index(max(shape))
    place[longest] = (place[longest] + 1) % shape[longest]
    return array.at[tuple(place)].set(largest)


def block_levels(stream_key, extent, cuts, low, top_value):
    loudness = 1.0
    for position, parts in cuts:
        draws = jax.random.uniform(jax.random.fold_in(jax.random.fold_in(stream_key, 6), position), (parts,), jnp.float32, low / len(cuts), top_value / len(cuts))
        loudness = loudness * jnp.repeat(jnp.exp(draws), extent[position] // parts).reshape((-1,) + (1,) * (len(extent) - 1 - position))
    return loudness


def normal_values(own_key, shape, width, limit, cuts=(), kind=jnp.bfloat16):
    drawn = jax.random.normal(own_key, shape, jnp.float32) * width
    if len(cuts) > 0:
        drawn = block_levels(own_key, shape, cuts, -0.22, 0.18) * drawn
    return jnp.clip(drawn, min=-limit, max=limit).astype(kind)


def setup_inputs(seed: int = 0) -> dict:
    key_list = jax.random.split(jax.random.key(seed), 9)
    return {
        "tokens": normal_values(key_list[0], (TOKENS, D), 1.0, 6.0, ((0, 256),), jnp.float32),
        "cotangent": normal_values(key_list[1], (TOKENS, D), 1.0, 6.0, ((0, 256),), jnp.float32),
        "w_gate": normal_values(key_list[2], (PIECES, D, HALF), D ** -0.5, 0.1875, ((0, 256),), jnp.float32),
        "w_up": normal_values(key_list[3], (PIECES, D, HALF), D ** -0.5, 0.1875, ((0, 256),), jnp.float32),
        "w_down": normal_values(key_list[4], (PIECES, HALF, D), HIDDEN_SIZE ** -0.5, 0.25, ((0, 256),), jnp.float32),
        "expert_ids": draw_expert_ids(jax.random.fold_in(key_list[8], 71), 0),
        "route_weight": jnp.clip(0.25 + 0.75 * jax.random.uniform(key_list[6], (TOKENS, 2), jnp.float32) ** block_levels(key_list[6], (TOKENS, 2), ((0, 256),), -0.2, 0.2), 0.25, 1.0),
        "halted": with_ends((jax.random.randint(key_list[7], (TOKENS,), 0, 4) < 1).astype(jnp.int32), jax.random.fold_in(key_list[7], 1), 0, 1),
    }


highest = lax.Precision.HIGHEST


def expert_grads(x_rows, d_rows, w_gate, w_upper, w_down):
    gate_value = jnp.dot(x_rows, w_gate, precision=highest)
    upper_value = jnp.dot(x_rows, w_upper, precision=highest)
    sigmoid_gate = jax.nn.sigmoid(gate_value)
    active = gate_value * sigmoid_gate
    hidden = active * upper_value
    d_hidden = jnp.dot(d_rows, w_down.T, precision=highest)
    d_gate = d_hidden * upper_value * sigmoid_gate * (1.0 + gate_value * (1.0 - sigmoid_gate))
    d_upper = d_hidden * active
    g_gate = jnp.dot(x_rows.T, d_gate, precision=highest)
    g_upper = jnp.dot(x_rows.T, d_upper, precision=highest)
    g_down = jnp.dot(hidden.T, d_rows, precision=highest)
    d_input = jnp.dot(d_gate, w_gate.T, precision=highest) + jnp.dot(d_upper, w_upper.T, precision=highest)
    return g_gate, g_upper, g_down, d_input


def reference(tokens, cotangent, w_gate, w_up, w_down, expert_ids, route_weight, halted):
    token_total, model_width = tokens.shape
    row_total = 2 * token_total
    capacity = N_EP * N_DP * MOST
    live_tokens = (1 - halted).astype(jnp.float32)
    route_rows = (route_weight * live_tokens[:, None]).reshape(-1)
    d_rows = jnp.repeat(cotangent, 2, axis=0) * route_rows[:, None]
    zero_row = jnp.zeros((1, model_width), jnp.float32)
    x_padded = jnp.concatenate([tokens, zero_row], axis=0)
    d_padded = jnp.concatenate([d_rows, zero_row], axis=0)
    gate_full = w_gate.reshape(EXPERTS, 2, model_width, HALF).transpose(0, 2, 1, 3).reshape(EXPERTS, model_width, HIDDEN_SIZE)
    upper_full = w_up.reshape(EXPERTS, 2, model_width, HALF).transpose(0, 2, 1, 3).reshape(EXPERTS, model_width, HIDDEN_SIZE)
    down_full = w_down.reshape(EXPERTS, HIDDEN_SIZE, model_width)
    flat_ids = expert_ids.reshape(-1)

    def one_expert(expert):
        picked = jnp.nonzero(flat_ids == expert, size=capacity, fill_value=row_total)[0].astype(jnp.int32)
        x_sel = x_padded[picked // 2]
        d_sel = d_padded[picked]
        g_gate, g_upper, g_down, d_input = expert_grads(x_sel, d_sel, gate_full[expert], upper_full[expert], down_full[expert])
        return g_gate, g_upper, g_down, d_input, picked

    g_gate, g_upper, g_down, d_input, picked = lax.map(one_expert, jnp.arange(EXPERTS, dtype=jnp.int32))
    summed = jnp.zeros((row_total + 1, model_width), jnp.float32).at[picked.reshape(-1)].add(d_input.reshape(-1, model_width))
    grad_x = cotangent + summed[:row_total].reshape(token_total, 2, model_width).sum(axis=1)
    grad_gate = g_gate.reshape(EXPERTS, model_width, 2, HALF).transpose(0, 2, 1, 3).reshape(PIECES, model_width, HALF)
    grad_up = g_upper.reshape(EXPERTS, model_width, 2, HALF).transpose(0, 2, 1, 3).reshape(PIECES, model_width, HALF)
    grad_down = g_down.reshape(PIECES, HALF, model_width)
    return grad_x, grad_gate, grad_up, grad_down
```

```python
import functools

import jax
import jax.numpy as jnp
from jax import lax
from jax.experimental import pallas as pl
from jax.experimental.pallas import tpu as pltpu
from jax.sharding import PartitionSpec as P

MESH = pl.DeviceIdType.MESH
MOST = 3
GROUPS = 4
LANES = 128
SUB = 8
F32 = jnp.float32
BF16 = jnp.bfloat16


def split(value):
    high = value.astype(BF16)
    return high, (value - high.astype(F32)).astype(BF16)


def dot3(a, b, a_dim, b_dim):
    def dot(p, q):
        return lax.dot_general(p, q, (((a_dim,), (b_dim,)), ((), ())), preferred_element_type=F32)

    return dot(a[0], b[0]) + dot(a[0], b[1]) + dot(a[1], b[0])


def kernel(
    nx,
    ny,
    nz,
    src_ref,
    wgt_ref,
    slot_ref,
    tok_ref,
    cot_ref,
    wg_ref,
    wu_ref,
    wd_ref,
    gx_ref,
    og_ref,
    ou_ref,
    od_ref,
    sbuf,
    rbuf,
    tbuf,
    bbuf,
    xg,
    xu,
    xd,
    gh,
    gl,
    uh,
    ul,
    dh,
    dl,
    ag,
    au,
    ad,
    rg,
    ru,
    rd,
    xh,
    xl,
    eh,
    el,
    send_sem,
    recv_sem,
    back_send_sem,
    back_recv_sem,
    pair_send_sem,
    pair_recv_sem,
):
    ep = lax.axis_index("ep")
    dp = lax.axis_index("dp")
    my_x, my_y = ep // ny, ep % ny
    my_z, my_c = dp // 2, dp % 2
    plane = nx * ny
    per_group = 2 * plane
    total = nz * plane
    half = wg_ref.shape[1]
    rows = per_group * MOST
    partner = (ep, my_z * 2 + 1 - my_c)

    def offset(k):
        group, low = k // per_group, k % per_group
        far, cell = low // plane, low % plane
        dz = (1 - far) * ((4 - group) % 4) + far * (4 + group)
        return cell // ny, cell % ny, dz

    def ahead(k):
        dx, dy, dz = offset(k)
        return ((my_x + dx) % nx) * ny + (my_y + dy) % ny, ((my_z + dz) % nz) * 2 + my_c

    def behind(k):
        dx, dy, dz = offset(k)
        return ((my_x + nx - dx) % nx) * ny + (my_y + ny - dy) % ny, ((my_z + nz - dz) % nz) * 2 + my_c

    barrier = pltpu.get_barrier_semaphore()

    @pl.loop(1, total)
    def _(k):
        pl.semaphore_signal(barrier, inc=1, device_id=ahead(k), device_id_type=MESH)

    pl.semaphore_signal(barrier, inc=1, device_id=partner, device_id_type=MESH)

    def gather(group):
        @pl.loop(0, per_group)
        def _(i):
            k = group * per_group + i
            for r in range(MOST):
                token = src_ref[k * MOST + r]
                sbuf[k, r] = tok_ref[token]
                sbuf[k, MOST + r] = cot_ref[token] * wgt_ref[k * MOST + r]

    def forward(k, group):
        return pltpu.make_async_remote_copy(
            src_ref=sbuf.at[k],
            dst_ref=rbuf.at[k],
            send_sem=send_sem,
            recv_sem=recv_sem.at[group],
            device_id=ahead(k),
            device_id_type=MESH,
        )

    def own_forward():
        return pltpu.make_async_copy(sbuf.at[0], rbuf.at[0], recv_sem.at[0])

    def send(group):
        @pl.loop(1 if group == 0 else 0, per_group)
        def _(i):
            forward(group * per_group + i, group).start()

        if group == 0:
            own_forward().start()

    def to_partner(i, src, dst):
        return pltpu.make_async_remote_copy(
            src_ref=src,
            dst_ref=dst,
            send_sem=pair_send_sem.at[i],
            recv_sem=pair_recv_sem.at[i],
            device_id=partner,
            device_id_type=MESH,
        )

    gather(0)
    gather(1)
    pl.semaphore_wait(barrier, total)
    send(0)
    gather(2)
    send(1)
    gather(3)
    send(2)

    weight_copies = [to_partner(0, wg_ref, xg), to_partner(1, wu_ref, xu), to_partner(2, wd_ref, xd)]
    for copy in weight_copies:
        copy.start()
    send(3)

    gh[:, :half], gl[:, :half] = split(wg_ref[...])
    uh[:, :half], ul[:, :half] = split(wu_ref[...])
    dh[:half, :], dl[:half, :] = split(wd_ref[...])
    for ref in (og_ref, ou_ref, od_ref, ag, au, ad):
        ref[...] = jnp.zeros_like(ref)
    for copy in weight_copies:
        copy.wait()
    gh[:, half:], gl[:, half:] = split(xg[...])
    uh[:, half:], ul[:, half:] = split(xu[...])
    dh[half:, :], dl[half:, :] = split(xd[...])

    flat_in = rbuf.reshape(total * 2 * MOST * SUB, LANES)
    flat_out = tbuf.reshape(total * MOST * SUB, LANES)

    def back(k):
        return pltpu.make_async_remote_copy(
            src_ref=tbuf.at[k],
            dst_ref=bbuf.at[k],
            send_sem=back_send_sem,
            recv_sem=back_recv_sem,
            device_id=behind(k),
            device_id_type=MESH,
        )

    def own_back():
        return pltpu.make_async_copy(tbuf.at[0], bbuf.at[0], back_recv_sem)

    @pl.loop(0, GROUPS)
    def _(group):
        first = group * per_group
        block = pl.ds(first, per_group)
        pltpu.make_async_copy(rbuf.at[block], rbuf.at[block], recv_sem.at[group]).wait()
        for r in range(MOST):
            for lane in range(xh.shape[1] // LANES):
                at = (pl.ds(r * per_group, per_group), pl.ds(lane * LANES, LANES))
                start = first * 2 * MOST * SUB + r * SUB + lane
                part = flat_in[pl.ds(start, per_group, stride=2 * MOST * SUB), :]
                xh[at], xl[at] = split(part)
                part = flat_in[pl.ds(start + MOST * SUB, per_group, stride=2 * MOST * SUB), :]
                eh[at], el[at] = split(part)
        x = (xh[...], xl[...])
        e = (eh[...], el[...])
        gate = dot3(x, (gh[...], gl[...]), 1, 0)
        upper = dot3(x, (uh[...], ul[...]), 1, 0)
        d_hidden = dot3(e, (dh[...], dl[...]), 1, 1)
        sig = jax.nn.sigmoid(gate)
        act = gate * sig
        hidden = split(act * upper)
        d_gate = split(d_hidden * upper * sig * (1.0 + gate * (1.0 - sig)))
        d_upper = split(d_hidden * act)
        d_in = dot3(d_gate, (gh[...], gl[...]), 1, 1) + dot3(d_upper, (uh[...], ul[...]), 1, 1)
        for r in range(MOST):
            for lane in range(xh.shape[1] // LANES):
                start = first * MOST * SUB + r * SUB + lane
                flat_out[pl.ds(start, per_group, stride=MOST * SUB), :] = d_in[
                    r * per_group : (r + 1) * per_group, lane * LANES : (lane + 1) * LANES
                ]
        d_gg = dot3(x, d_gate, 0, 0)
        d_uu = dot3(x, d_upper, 0, 0)
        d_dd = dot3(hidden, e, 0, 0)
        ag[...] += d_gg[:, half:]
        au[...] += d_uu[:, half:]
        ad[...] += d_dd[half:, :]
        og_ref[...] += d_gg[:, :half]
        ou_ref[...] += d_uu[:, :half]
        od_ref[...] += d_dd[:half, :]

        @pl.when(group == 0)
        def _():
            own_back().start()

        @pl.loop(jnp.where(group == 0, 1, 0), per_group)
        def _(i):
            back(first + i).start()

    grad_copies = [to_partner(3, ag, rg), to_partner(4, au, ru), to_partner(5, ad, rd)]
    for copy in grad_copies:
        copy.start()
    for copy, out, got in zip(grad_copies, (og_ref, ou_ref, od_ref), (rg, ru, rd)):
        copy.wait()
        out[...] += got[...]

    pltpu.make_async_copy(bbuf, bbuf, back_recv_sem).wait()

    @pl.loop(0, tok_ref.shape[0])
    def _(t):
        first, second = slot_ref[2 * t], slot_ref[2 * t + 1]
        a = bbuf[first // MOST, first % MOST]
        b = bbuf[second // MOST, second % MOST]
        gx_ref[t] = cot_ref[t] + (a + b)

    others = pl.ds(1, total - 1)
    pltpu.make_async_copy(sbuf.at[others], sbuf.at[others], send_sem).wait()
    pltpu.make_async_copy(tbuf.at[others], tbuf.at[others], back_send_sem).wait()


def local(nx, ny, nz, tokens, cotangent, w_gate, w_up, w_down, expert_ids, route_weight, halted):
    token_count, width = tokens.shape
    half = w_gate.shape[2]
    plane = nx * ny
    total = nx * ny * nz
    slots = total * MOST
    ep = lax.axis_index("ep")
    my_z = lax.axis_index("dp") // 2
    expert = expert_ids.reshape(-1)
    pairs = expert.shape[0]
    row = jnp.arange(pairs, dtype=jnp.int32)
    earlier = (expert[:, None] == expert[None, :]) & (row[None, :] < row[:, None])
    rank = jnp.sum(earlier.astype(jnp.int32), axis=1)
    to_ep, to_z = expert // nz, expert % nz
    dx = (to_ep // ny - ep // ny + nx) % nx
    dy = (to_ep % ny - ep % ny + ny) % ny
    dz = (to_z - my_z + nz) % nz
    group = jnp.where(dz >= 4, dz - 4, (4 - dz) % 4)
    far = jnp.where(dz >= 4, 1, 0)
    place = group * (2 * plane) + far * plane + dx * ny + dy
    slot = place * MOST + rank
    hit = slot[None, :] == jnp.arange(slots, dtype=jnp.int32)[:, None]
    weight = (route_weight * (1 - halted).astype(F32)[:, None]).reshape(-1)
    src = jnp.sum(jnp.where(hit, (row // 2)[None, :], 0), axis=1)
    wgt = jnp.sum(jnp.where(hit, weight[None, :], 0.0), axis=1)
    per_group = 2 * plane
    rows = per_group * MOST
    tile = (SUB, LANES)
    vmem = pl.BlockSpec(memory_space=pltpu.VMEM)
    smem = pl.BlockSpec(memory_space=pltpu.SMEM)
    grad_x, g_gate, g_upper, g_down = pl.pallas_call(
        functools.partial(kernel, nx, ny, nz),
        out_shape=(
            jax.ShapeDtypeStruct((token_count,) + tile, F32),
            jax.ShapeDtypeStruct((width, half), F32),
            jax.ShapeDtypeStruct((width, half), F32),
            jax.ShapeDtypeStruct((half, width), F32),
        ),
        in_specs=[smem, smem, smem] + [vmem] * 5,
        out_specs=(vmem,) * 4,
        scratch_shapes=[
            pltpu.VMEM((total, 2 * MOST) + tile, F32),
            pltpu.VMEM((total, 2 * MOST) + tile, F32),
            pltpu.VMEM((total, MOST) + tile, F32),
            pltpu.VMEM((total, MOST) + tile, F32),
            pltpu.VMEM((width, half), F32),
            pltpu.VMEM((width, half), F32),
            pltpu.VMEM((half, width), F32),
            pltpu.VMEM((width, 2 * half), BF16),
            pltpu.VMEM((width, 2 * half), BF16),
            pltpu.VMEM((width, 2 * half), BF16),
            pltpu.VMEM((width, 2 * half), BF16),
            pltpu.VMEM((2 * half, width), BF16),
            pltpu.VMEM((2 * half, width), BF16),
            pltpu.VMEM((width, half), F32),
            pltpu.VMEM((width, half), F32),
            pltpu.VMEM((half, width), F32),
            pltpu.VMEM((width, half), F32),
            pltpu.VMEM((width, half), F32),
            pltpu.VMEM((half, width), F32),
            pltpu.VMEM((rows, width), BF16),
            pltpu.VMEM((rows, width), BF16),
            pltpu.VMEM((rows, width), BF16),
            pltpu.VMEM((rows, width), BF16),
            pltpu.SemaphoreType.DMA,
            pltpu.SemaphoreType.DMA((GROUPS,)),
            pltpu.SemaphoreType.DMA,
            pltpu.SemaphoreType.DMA,
            pltpu.SemaphoreType.DMA((6,)),
            pltpu.SemaphoreType.DMA((6,)),
        ],
        compiler_params=pltpu.CompilerParams(
            collective_id=0, has_side_effects=True, vmem_limit_bytes=63 * 1024 * 1024
        ),
    )(
        src,
        wgt,
        slot,
        tokens.reshape((token_count,) + tile),
        cotangent.reshape((token_count,) + tile),
        w_gate[0],
        w_up[0],
        w_down[0],
    )
    return grad_x.reshape(token_count, width), g_gate[None], g_upper[None], g_down[None]


def solution(mesh):
    nx, ny = 4, 4
    nz = mesh.shape["dp"] // 2
    spec2 = P(("ep", "dp"), None)
    spec3 = P(("ep", "dp"), None, None)
    return jax.shard_map(
        functools.partial(local, nx, ny, nz),
        mesh=mesh,
        in_specs=(spec2, spec2, spec3, spec3, spec3, spec2, spec2, P(("ep", "dp"))),
        out_specs=(spec2, spec3, spec3, spec3),
        check_vma=False,
    )
```

```python
import functools

import jax
import jax.numpy as jnp
from jax import lax
from jax.experimental import pallas as pl
from jax.experimental.pallas import tpu as pltpu
from jax.sharding import PartitionSpec as P

MESH = pl.DeviceIdType.MESH
MOST = 3
GROUPS = 4
FIRST = 48
CAPS = ((128, 128, 96, 48), (128, 96, 48))
LANES = 128
SUB = 8
F32 = jnp.float32
BF16 = jnp.bfloat16


def split(value):
    high = value.astype(BF16)
    return high, (value - high.astype(F32)).astype(BF16)


def dot3(a, b, a_dim, b_dim):
    def dot(p, q):
        return lax.dot_general(p, q, (((a_dim,), (b_dim,)), ((), ())), preferred_element_type=F32)

    return dot(a[0], b[0]) + dot(a[0], b[1]) + dot(a[1], b[0])


def kernel(
    nx,
    ny,
    nz,
    ids_ref,
    route_ref,
    halt_ref,
    tok_ref,
    cot_ref,
    wg_ref,
    wu_ref,
    wd_ref,
    gx_ref,
    og_ref,
    ou_ref,
    od_ref,
    tok3,
    cot3,
    turn_a,
    turn_b,
    turn_w,
    list_v,
    list_s,
    row_ref,
    wgt_ref,
    own,
    hops,
    row_in,
    wgt_in,
    row_tab,
    wgt_tab,
    sbuf,
    rbuf,
    tbuf,
    bbuf,
    xg,
    xu,
    xd,
    gh,
    gl,
    uh,
    ul,
    dh,
    dl,
    ag,
    au,
    ad,
    rg,
    ru,
    rd,
    xh,
    xl,
    eh,
    el,
    hop_send_sem,
    hop_recv_sem,
    row_send_sem,
    row_recv_sem,
    wgt_send_sem,
    wgt_recv_sem,
    tab_sem,
    send_sem,
    recv_sem,
    back_send_sem,
    back_recv_sem,
    pair_send_sem,
    pair_recv_sem,
):
    ep = lax.axis_index("ep")
    dp = lax.axis_index("dp")
    my_x, my_y = ep // ny, ep % ny
    my_z, my_c = dp // 2, dp % 2
    sign = 1 - 2 * my_c
    plane = nx * ny
    per_group = 2 * plane
    total = nz * plane
    half = wg_ref.shape[1]
    tokens, width = tok_ref.shape
    low_bits = nz - 1
    partner = (ep, my_z * 2 + 1 - my_c)

    def column(step):
        return ep, ((my_z + nz + step) % nz) * 2 + my_c

    def offset(k):
        group, low = k // per_group, k % per_group
        side, cell = low // plane, low % plane
        hop = group + 1
        dz = jnp.where(side == 0, sign * hop, jnp.where(group == GROUPS - 1, 0, -sign * hop))
        return cell // ny, cell % ny, dz

    def behind(k):
        dx, dy, dz = offset(k)
        return ((my_x + nx - dx) % nx) * ny + (my_y + ny - dy) % ny, ((my_z + nz - dz) % nz) * 2 + my_c

    def beside(cell):
        return ((my_x + cell // ny) % nx) * ny + (my_y + cell % ny) % ny, dp

    barrier = pltpu.get_barrier_semaphore()

    @pl.loop(0, nz)
    def _(other_z):
        @pl.loop(0, plane)
        def _(other):
            @pl.when((other_z != my_z) | (other != ep))
            def _():
                pl.semaphore_signal(barrier, inc=1, device_id=(other, other_z * 2 + my_c), device_id_type=MESH)

    pl.semaphore_signal(barrier, inc=1, device_id=partner, device_id_type=MESH)

    def remote(src, dst, send, recv, device):
        return pltpu.make_async_remote_copy(
            src_ref=src, dst_ref=dst, send_sem=send, recv_sem=recv, device_id=device, device_id_type=MESH
        )

    def toward(side):
        return column(sign if side == 0 else -sign)

    def hop_parts(side, hop):
        cap = CAPS[side][hop]
        return ((0, FIRST), (FIRST, cap)) if cap > FIRST else ((0, cap),)

    def hop_copy(side, hop, part):
        start, end = hop_parts(side, hop)[part]
        rows = pl.ds(start, end - start)
        src = own.at[side, rows] if hop == 0 else hops[side][hop - 1].at[rows]
        return remote(
            src,
            hops[side][hop].at[rows],
            hop_send_sem.at[side, hop, part],
            hop_recv_sem.at[side, hop, part],
            toward(side),
        )

    def table_copies(side, hop):
        device = column(sign * (hop + 1) if side == 0 else -sign * (hop + 1))
        at = 2 * hop + side
        return (
            remote(row_ref.at[at], row_in.at[side, hop], row_send_sem.at[at], row_recv_sem.at[side, hop], device),
            remote(wgt_ref.at[at], wgt_in.at[side, hop], wgt_send_sem.at[at], wgt_recv_sem.at[side, hop], device),
        )

    def block_copy(k, group, cell):
        return remote(sbuf.at[k], rbuf.at[k], send_sem, recv_sem.at[group], beside(cell))

    def send_blocks(group, side):
        first = group * per_group + side * plane
        pltpu.make_async_copy(sbuf.at[first], rbuf.at[first], recv_sem.at[group]).start()

        @pl.loop(1, plane)
        def _(cell):
            block_copy(first + cell, group, cell).start()

    def to_partner(i, src, dst):
        return remote(src, dst, pair_send_sem.at[i], pair_recv_sem.at[i], partner)

    flat_tok = tok3.reshape(tokens * SUB, LANES)
    flat_cot = cot3.reshape(tokens * SUB, LANES)
    for lane in range(SUB):
        at = pl.ds(lane * LANES, LANES)
        to = pl.ds(lane, tokens, stride=SUB)
        flat_tok[to, :] = tok_ref[:, at]
        flat_cot[to, :] = cot_ref[:, at]

    live = 1 - halt_ref[...]
    experts = [ids_ref[pl.ds(j, 1), :] for j in range(2)]
    turned = [(sign * ((e & low_bits) - my_z)) & low_bits for e in experts]
    long_side = [(t >= 1) & (t <= GROUPS) for t in turned]
    short_side = [t > GROUPS for t in turned]
    far = [
        jnp.maximum(*[jnp.where(m, t, 0) for m, t in zip(long_side, turned)]) * live,
        jnp.maximum(*[jnp.where(m, nz - t, 0) for m, t in zip(short_side, turned)]) * live,
    ]
    for ref in (turn_a, turn_b, turn_w):
        ref[...] = jnp.zeros_like(ref)
    list_v[...] = jnp.zeros_like(list_v)
    for i, line in enumerate(experts + far):
        turn_a[pl.ds(i, 1), :] = line
    columns = turn_a[...].T
    below = lax.broadcasted_iota(jnp.int32, (tokens, tokens), 0)
    across = lax.broadcasted_iota(jnp.int32, (tokens, tokens), 1)
    earlier = below < across

    def column_of(matrix, i):
        return matrix[:, i : i + 1]

    def count(mask):
        return jnp.sum(jnp.where(mask, 1, 0), axis=0, keepdims=True)

    lines = [turn_a[pl.ds(i, 1), :] for i in range(4)]
    ranks = [
        count((column_of(columns, 0) == lines[0]) & earlier),
        count((column_of(columns, 1) == lines[1]) & earlier) + count(column_of(columns, 0) == lines[1]),
    ]
    places = []
    for i in (2, 3):
        other = column_of(columns, i)
        places.append(count((other > lines[i]) | ((other == lines[i]) & earlier)))
    lane_index = lax.broadcasted_iota(jnp.int32, (1, tokens), 1)
    shift = nz.bit_length() - 1
    for i in range(2):
        turn_b[pl.ds(i, 1), :] = places[i]
    for j in range(2):
        to_ep = experts[j] >> shift
        dx = ((to_ep >> (ny.bit_length() - 1)) - my_x) & (nx - 1)
        dy = ((to_ep & (ny - 1)) - my_y) & (ny - 1)
        hop = jnp.where(long_side[j], turned[j] - 1, jnp.where(turned[j] == 0, GROUPS - 1, nz - 1 - turned[j]))
        line = 2 * hop + jnp.where(long_side[j], 0, 1)
        within = (dx * ny + dy) * MOST + jnp.minimum(ranks[j], MOST - 1)
        list_v[pl.ds(2 + j, 1), :] = jnp.clip(line * (plane * MOST) + within, 0, total * MOST - 1)
        row = jnp.where(long_side[j], places[0], jnp.where(turned[j] == 0, lane_index, places[1]))
        turn_b[pl.ds(2 + j, 1), :] = line * LANES + within
        turn_b[pl.ds(4 + j, 1), :] = row * live
        turn_w[pl.ds(j, 1), :] = route_ref[pl.ds(j, 1), :] * live.astype(F32)
    columns = turn_b[...].T
    weights = turn_w[...].T
    for i in range(2):
        found = jnp.sum(jnp.where(column_of(columns, i) == across, below, 0), axis=0, keepdims=True)
        list_v[pl.ds(i, 1), :] = jnp.clip(found, 0, tokens - 1)
    pick_lists = pltpu.make_async_copy(list_v, list_s, tab_sem.at[0])
    pick_lists.start()
    for i in range(2 * GROUPS):
        hit = [column_of(columns, 2 + j) == across + i * LANES for j in range(2)]
        row = jnp.sum(
            sum(jnp.where(hit[j], column_of(columns, 4 + j), 0) for j in range(2)), axis=0, keepdims=True
        )
        wgt = jnp.sum(
            sum(jnp.where(hit[j], column_of(weights, j), 0.0) for j in range(2)), axis=0, keepdims=True
        )
        limit = CAPS[i % 2][i // 2] if i // 2 < len(CAPS[i % 2]) else tokens
        row_ref[i] = jnp.broadcast_to(jnp.clip(row, 0, limit - 1), (SUB, LANES))
        wgt_ref[i] = jnp.broadcast_to(wgt, (SUB, LANES))
    pick_lists.wait()

    @pl.loop(0, tokens // SUB)
    def _(block):
        for side in range(2):
            picked = [list_s[side, block * SUB + i] for i in range(SUB)]
            rows = [(tok3[token], cot3[token]) for token in picked]
            for i, (a, b) in enumerate(rows):
                own[side, block * SUB + i, 0] = a
                own[side, block * SUB + i, 1] = b

    last_line = 2 * GROUPS - 1
    own_tables = [
        pltpu.make_async_copy(row_ref.at[last_line], row_tab.at[1, GROUPS - 1], tab_sem.at[0]),
        pltpu.make_async_copy(wgt_ref.at[last_line], wgt_tab.at[1, GROUPS - 1], tab_sem.at[1]),
    ]
    for copy in own_tables:
        copy.start()
    pl.semaphore_wait(barrier, total)
    lanes = [(side, hop) for hop in range(GROUPS) for side in range(2) if hop < len(CAPS[side])]
    for part in range(2):
        for side in range(2):
            hop_copy(side, 0, part).start()
    for side, hop in lanes:
        for copy in table_copies(side, hop):
            copy.start()
    weight_copies = [to_partner(0, wg_ref, xg), to_partner(1, wu_ref, xu), to_partner(2, wd_ref, xd)]
    for copy in weight_copies:
        copy.start()
    for copy in own_tables:
        copy.wait()

    def pick(group, side):
        held = None if (group, side) == (GROUPS - 1, 1) else hops[side][group]

        @pl.loop(0, plane)
        def _(cell):
            k = group * per_group + side * plane + cell
            at = [(row_tab[side, group, 0, cell * MOST + r], wgt_tab[side, group, 0, cell * MOST + r]) for r in range(MOST)]
            if held is None:
                rows = [(tok3[row], cot3[row] * wgt) for row, wgt in at]
            else:
                rows = [(held[row, 0], held[row, 1] * wgt) for row, wgt in at]
            for r, (a, b) in enumerate(rows):
                sbuf[k, r] = a
                sbuf[k, MOST + r] = b

    pick(GROUPS - 1, 1)
    send_blocks(GROUPS - 1, 1)

    gh[:, :half], gl[:, :half] = split(wg_ref[...])
    uh[:, :half], ul[:, :half] = split(wu_ref[...])
    dh[:half, :], dl[:half, :] = split(wd_ref[...])
    for ref in (og_ref, ou_ref, od_ref, ag, au, ad):
        ref[...] = jnp.zeros_like(ref)
    for copy in weight_copies:
        copy.wait()
    gh[:, half:], gl[:, half:] = split(xg[...])
    uh[:, half:], ul[:, half:] = split(xu[...])
    dh[half:, :], dl[half:, :] = split(xd[...])
    for side, hop in lanes:
        for copy in table_copies(side, hop):
            copy.wait_recv()
    tables = [
        pltpu.make_async_copy(table.at[side, pl.ds(0, len(CAPS[side]))], to.at[side, pl.ds(0, len(CAPS[side]))], tab_sem.at[i])
        for i, (table, to, side) in enumerate(
            [(row_in, row_tab, 0), (wgt_in, wgt_tab, 0), (row_in, row_tab, 1), (wgt_in, wgt_tab, 1)]
        )
    ]
    for copy in tables:
        copy.start()
    for copy in tables:
        copy.wait()

    flat_in = rbuf.reshape(total * 2 * MOST * SUB, LANES)
    flat_out = tbuf.reshape(total * MOST * SUB, LANES)

    def back(k):
        return remote(tbuf.at[k], bbuf.at[k], back_send_sem, back_recv_sem, behind(k))

    def compute(group):
        first = group * per_group
        block = pl.ds(first, per_group)
        pltpu.make_async_copy(rbuf.at[block], rbuf.at[block], recv_sem.at[group]).wait()
        for r in range(MOST):
            for lane in range(xh.shape[1] // LANES):
                at = (pl.ds(r * per_group, per_group), pl.ds(lane * LANES, LANES))
                start = first * 2 * MOST * SUB + r * SUB + lane
                part = flat_in[pl.ds(start, per_group, stride=2 * MOST * SUB), :]
                xh[at], xl[at] = split(part)
                part = flat_in[pl.ds(start + MOST * SUB, per_group, stride=2 * MOST * SUB), :]
                eh[at], el[at] = split(part)
        x = (xh[...], xl[...])
        e = (eh[...], el[...])
        gate = dot3(x, (gh[...], gl[...]), 1, 0)
        upper = dot3(x, (uh[...], ul[...]), 1, 0)
        d_hidden = dot3(e, (dh[...], dl[...]), 1, 1)
        sig = jax.nn.sigmoid(gate)
        act = gate * sig
        hidden = split(act * upper)
        d_gate = split(d_hidden * upper * sig * (1.0 + gate * (1.0 - sig)))
        d_upper = split(d_hidden * act)
        d_in = dot3(d_gate, (gh[...], gl[...]), 1, 1) + dot3(d_upper, (uh[...], ul[...]), 1, 1)
        for r in range(MOST):
            for lane in range(xh.shape[1] // LANES):
                start = first * MOST * SUB + r * SUB + lane
                flat_out[pl.ds(start, per_group, stride=MOST * SUB), :] = d_in[
                    r * per_group : (r + 1) * per_group, lane * LANES : (lane + 1) * LANES
                ]
        d_gg = dot3(x, d_gate, 0, 0)
        d_uu = dot3(x, d_upper, 0, 0)
        d_dd = dot3(hidden, e, 0, 0)
        ag[...] += d_gg[:, half:]
        au[...] += d_uu[:, half:]
        ad[...] += d_dd[half:, :]
        og_ref[...] += d_gg[:, :half]
        ou_ref[...] += d_uu[:, :half]
        od_ref[...] += d_dd[:half, :]

        own_block = (GROUPS - 1) * per_group + plane

        @pl.loop(0, per_group)
        def _(i):
            k = first + i

            @pl.when(k != own_block)
            def _():
                back(k).start()

            @pl.when(k == own_block)
            def _():
                pltpu.make_async_copy(tbuf.at[own_block], bbuf.at[own_block], back_recv_sem).start()

    @pl.loop(0, GROUPS + 1)
    def _(step):
        for hop in range(GROUPS):

            @pl.when(step == hop)
            def _():
                for side in range(2):
                    if hop < len(CAPS[side]):
                        for part in range(len(hop_parts(side, hop))):
                            hop_copy(side, hop, part).wait_recv()
                            if hop + 1 < len(CAPS[side]) and part < len(hop_parts(side, hop + 1)):
                                hop_copy(side, hop + 1, part).start()
                for side in range(2):
                    if hop < len(CAPS[side]):
                        pick(hop, side)
                for side in range(2):
                    if hop < len(CAPS[side]):
                        send_blocks(hop, side)

        @pl.when(step >= 1)
        def _():
            compute(step - 1)

    grad_copies = [to_partner(3, ag, rg), to_partner(4, au, ru), to_partner(5, ad, rd)]
    for copy in grad_copies:
        copy.start()
    for copy, out, got in zip(grad_copies, (og_ref, ou_ref, od_ref), (rg, ru, rd)):
        copy.wait()
        out[...] += got[...]

    pltpu.make_async_copy(bbuf, bbuf, back_recv_sem).wait()

    flat_back = bbuf.reshape(total * MOST, SUB, LANES)

    @pl.loop(0, tokens // SUB)
    def _(block):
        found = []
        for i in range(SUB):
            t = block * SUB + i
            found.append(cot3[t] + (flat_back[list_s[2, t]] + flat_back[list_s[3, t]]))
        for i, value in enumerate(found):
            tok3[block * SUB + i] = value

    for lane in range(SUB):
        gx_ref[:, pl.ds(lane * LANES, LANES)] = flat_tok[pl.ds(lane, tokens, stride=SUB), :]

    for side, hop in lanes:
        for part in range(len(hop_parts(side, hop))):
            hop_copy(side, hop, part).wait_send()
        for copy in table_copies(side, hop):
            copy.wait_send()
    sent = pl.ds(0, total - 2 * GROUPS)
    pltpu.make_async_copy(sbuf.at[sent], sbuf.at[sent], send_sem).wait()
    others = pl.ds(0, total - 1)
    pltpu.make_async_copy(tbuf.at[others], tbuf.at[others], back_send_sem).wait()


def local(nx, ny, nz, tokens, cotangent, w_gate, w_up, w_down, expert_ids, route_weight, halted):
    token_count, width = tokens.shape
    half = w_gate.shape[2]
    plane = nx * ny
    total = nx * ny * nz
    rows = 2 * plane * MOST
    tile = (SUB, LANES)
    vmem = pl.BlockSpec(memory_space=pltpu.VMEM)
    dma = pltpu.SemaphoreType.DMA
    grad_x, g_gate, g_upper, g_down = pl.pallas_call(
        functools.partial(kernel, nx, ny, nz),
        out_shape=(
            jax.ShapeDtypeStruct((token_count, width), F32),
            jax.ShapeDtypeStruct((width, half), F32),
            jax.ShapeDtypeStruct((width, half), F32),
            jax.ShapeDtypeStruct((half, width), F32),
        ),
        in_specs=[vmem] * 8,
        out_specs=(vmem,) * 4,
        scratch_shapes=[
            pltpu.VMEM((token_count,) + tile, F32),
            pltpu.VMEM((token_count,) + tile, F32),
            pltpu.VMEM(tile, jnp.int32),
            pltpu.VMEM(tile, jnp.int32),
            pltpu.VMEM(tile, F32),
            pltpu.VMEM(tile, jnp.int32),
            pltpu.SMEM(tile, jnp.int32),
            pltpu.VMEM((2 * GROUPS,) + tile, jnp.int32),
            pltpu.VMEM((2 * GROUPS,) + tile, F32),
            pltpu.VMEM((2, token_count, 2) + tile, F32),
            tuple(tuple(pltpu.VMEM((cap, 2) + tile, F32) for cap in caps) for caps in CAPS),
            pltpu.VMEM((2, GROUPS) + tile, jnp.int32),
            pltpu.VMEM((2, GROUPS) + tile, F32),
            pltpu.SMEM((2, GROUPS) + tile, jnp.int32),
            pltpu.SMEM((2, GROUPS) + tile, F32),
            pltpu.VMEM((total, 2 * MOST) + tile, F32),
            pltpu.VMEM((total, 2 * MOST) + tile, F32),
            pltpu.VMEM((total, MOST) + tile, F32),
            pltpu.VMEM((total, MOST) + tile, F32),
            pltpu.VMEM((width, half), F32),
            pltpu.VMEM((width, half), F32),
            pltpu.VMEM((half, width), F32),
            pltpu.VMEM((width, 2 * half), BF16),
            pltpu.VMEM((width, 2 * half), BF16),
            pltpu.VMEM((width, 2 * half), BF16),
            pltpu.VMEM((width, 2 * half), BF16),
            pltpu.VMEM((2 * half, width), BF16),
            pltpu.VMEM((2 * half, width), BF16),
            pltpu.VMEM((width, half), F32),
            pltpu.VMEM((width, half), F32),
            pltpu.VMEM((half, width), F32),
            pltpu.VMEM((width, half), F32),
            pltpu.VMEM((width, half), F32),
            pltpu.VMEM((half, width), F32),
            pltpu.VMEM((rows, width), BF16),
            pltpu.VMEM((rows, width), BF16),
            pltpu.VMEM((rows, width), BF16),
            pltpu.VMEM((rows, width), BF16),
            dma((2, GROUPS, 2)),
            dma((2, GROUPS, 2)),
            dma((2 * GROUPS,)),
            dma((2, GROUPS)),
            dma((2 * GROUPS,)),
            dma((2, GROUPS)),
            dma((4,)),
            dma,
            dma((GROUPS,)),
            dma,
            dma,
            dma((6,)),
            dma((6,)),
        ],
        compiler_params=pltpu.CompilerParams(
            collective_id=0, has_side_effects=True, vmem_limit_bytes=63 * 1024 * 1024
        ),
    )(
        expert_ids.T,
        route_weight.T,
        halted.reshape(1, token_count),
        tokens,
        cotangent,
        w_gate[0],
        w_up[0],
        w_down[0],
    )
    return grad_x, g_gate[None], g_upper[None], g_down[None]


def solution(mesh):
    nx, ny = 4, 4
    nz = mesh.shape["dp"] // 2
    spec2 = P(("ep", "dp"), None)
    spec3 = P(("ep", "dp"), None, None)
    return jax.shard_map(
        functools.partial(local, nx, ny, nz),
        mesh=mesh,
        in_specs=(spec2, spec2, spec3, spec3, spec3, spec2, spec2, P(("ep", "dp"))),
        out_specs=(spec2, spec3, spec3, spec3),
        check_vma=False,
    )
```

```python
import functools

import jax
import jax.numpy as jnp
from jax import lax
from jax.experimental import pallas as pl
from jax.experimental.pallas import tpu as pltpu
from jax.sharding import PartitionSpec as P

MESH = pl.DeviceIdType.MESH
MOST = 3
GROUPS = 4
FIRST = 48
CAPS = ((128, 128, 96, 48), (128, 96, 48))
LANES = 128
SUB = 8
F32 = jnp.float32
BF16 = jnp.bfloat16


def split(value):
    high = value.astype(BF16)
    return high, (value - high.astype(F32)).astype(BF16)


def dot3(a, b, a_dim, b_dim):
    def dot(p, q):
        return lax.dot_general(p, q, (((a_dim,), (b_dim,)), ((), ())), preferred_element_type=F32)

    return dot(a[0], b[0]) + dot(a[0], b[1]) + dot(a[1], b[0])


def kernel(
    nx,
    ny,
    nz,
    ids_ref,
    route_ref,
    halt_ref,
    tok_ref,
    cot_ref,
    wg_ref,
    wu_ref,
    wd_ref,
    gx_ref,
    og_ref,
    ou_ref,
    od_ref,
    wg,
    wu,
    wd,
    og,
    ou,
    od,
    tok3,
    cot3,
    turn_a,
    turn_b,
    turn_w,
    list_v,
    list_s,
    row_ref,
    wgt_ref,
    own,
    hops,
    row_in,
    wgt_in,
    row_tab,
    wgt_tab,
    sbuf,
    rbuf,
    tbuf,
    bbuf,
    xg,
    xu,
    xd,
    gh,
    gl,
    uh,
    ul,
    dh,
    dl,
    ag,
    au,
    ad,
    rg,
    ru,
    rd,
    xh,
    xl,
    eh,
    el,
    load_sem,
    meet_sem,
    hop_send_sem,
    hop_recv_sem,
    row_send_sem,
    row_recv_sem,
    wgt_send_sem,
    wgt_recv_sem,
    tab_sem,
    send_sem,
    recv_sem,
    back_send_sem,
    back_recv_sem,
    pair_send_sem,
    pair_recv_sem,
):
    ep = lax.axis_index("ep")
    dp = lax.axis_index("dp")
    my_x, my_y = ep // ny, ep % ny
    my_z, my_c = dp // 2, dp % 2
    sign = 1 - 2 * my_c
    plane = nx * ny
    per_group = 2 * plane
    total = nz * plane
    half = wg.shape[1]
    tokens, width = tok_ref.shape
    low_bits = nz - 1
    partner = (ep, my_z * 2 + 1 - my_c)

    def column(step):
        return ep, ((my_z + nz + step) % nz) * 2 + my_c

    def offset(k):
        group, low = k // per_group, k % per_group
        side, cell = low // plane, low % plane
        hop = group + 1
        dz = jnp.where(side == 0, sign * hop, jnp.where(group == GROUPS - 1, 0, -sign * hop))
        return cell // ny, cell % ny, dz

    def behind(k):
        dx, dy, dz = offset(k)
        return ((my_x + nx - dx) % nx) * ny + (my_y + ny - dy) % ny, ((my_z + nz - dz) % nz) * 2 + my_c

    def beside(cell):
        return ((my_x + cell // ny) % nx) * ny + (my_y + cell % ny) % ny, dp

    barrier = pltpu.get_barrier_semaphore()

    def at_xy(dx, dy):
        return ((my_x + nx + dx) % nx) * ny + (my_y + ny + dy) % ny, dp

    rings = (
        (column(1), column(-1)),
        (at_xy(1, 0), at_xy(-1, 0)),
        (at_xy(0, 1), at_xy(0, -1)),
    )
    for device in [device for ring in rings for device in ring] + [partner]:
        pl.semaphore_signal(barrier, inc=1, device_id=device, device_id_type=MESH)

    weight_loads = [
        pltpu.make_async_copy(src, dst, load_sem.at[i])
        for i, (src, dst) in enumerate([(wg_ref, wg), (wu_ref, wu), (wd_ref, wd)])
    ]
    for copy in weight_loads:
        copy.start()

    def meet():
        turn = 0
        for ring, length in zip(rings, (nz, nx, ny)):
            for _ in range(length // 2 - (1 if length == nz else 0)):
                for device in ring:
                    pl.semaphore_signal(meet_sem.at[turn], inc=1, device_id=device, device_id_type=MESH)
                pl.semaphore_wait(meet_sem.at[turn], 2)
                turn += 1

    def remote(src, dst, send, recv, device):
        return pltpu.make_async_remote_copy(
            src_ref=src, dst_ref=dst, send_sem=send, recv_sem=recv, device_id=device, device_id_type=MESH
        )

    def toward(side):
        return column(sign if side == 0 else -sign)

    def hop_parts(side, hop):
        cap = CAPS[side][hop]
        return ((0, FIRST), (FIRST, cap)) if cap > FIRST else ((0, cap),)

    def hop_copy(side, hop, part):
        start, end = hop_parts(side, hop)[part]
        rows = pl.ds(start, end - start)
        src = own.at[side, rows] if hop == 0 else hops[side][hop - 1].at[rows]
        return remote(
            src,
            hops[side][hop].at[rows],
            hop_send_sem.at[side, hop, part],
            hop_recv_sem.at[side, hop, part],
            toward(side),
        )

    def table_copies(side, hop):
        device = column(sign * (hop + 1) if side == 0 else -sign * (hop + 1))
        at = 2 * hop + side
        return (
            remote(row_ref.at[at], row_in.at[side, hop], row_send_sem.at[at], row_recv_sem.at[side, hop], device),
            remote(wgt_ref.at[at], wgt_in.at[side, hop], wgt_send_sem.at[at], wgt_recv_sem.at[side, hop], device),
        )

    def block_copy(k, group, cell):
        return remote(sbuf.at[k], rbuf.at[k], send_sem, recv_sem.at[group], beside(cell))

    def send_blocks(group, side):
        first = group * per_group + side * plane
        pltpu.make_async_copy(sbuf.at[first], rbuf.at[first], recv_sem.at[group]).start()

        @pl.loop(1, plane)
        def _(cell):
            block_copy(first + cell, group, cell).start()

    def to_partner(i, src, dst):
        return remote(src, dst, pair_send_sem.at[i], pair_recv_sem.at[i], partner)

    flat_tok = tok3.reshape(tokens * SUB, LANES)
    flat_cot = cot3.reshape(tokens * SUB, LANES)
    for lane in range(SUB):
        at = pl.ds(lane * LANES, LANES)
        to = pl.ds(lane, tokens, stride=SUB)
        flat_tok[to, :] = tok_ref[:, at]
        flat_cot[to, :] = cot_ref[:, at]

    live = 1 - halt_ref[...]
    experts = [ids_ref[pl.ds(j, 1), :] for j in range(2)]
    turned = [(sign * ((e & low_bits) - my_z)) & low_bits for e in experts]
    long_side = [(t >= 1) & (t <= GROUPS) for t in turned]
    short_side = [t > GROUPS for t in turned]
    far = [
        jnp.maximum(*[jnp.where(m, t, 0) for m, t in zip(long_side, turned)]) * live,
        jnp.maximum(*[jnp.where(m, nz - t, 0) for m, t in zip(short_side, turned)]) * live,
    ]
    for ref in (turn_a, turn_b, turn_w):
        ref[...] = jnp.zeros_like(ref)
    list_v[...] = jnp.zeros_like(list_v)
    for i, line in enumerate(experts + far):
        turn_a[pl.ds(i, 1), :] = line
    columns = turn_a[...].T
    below = lax.broadcasted_iota(jnp.int32, (tokens, tokens), 0)
    across = lax.broadcasted_iota(jnp.int32, (tokens, tokens), 1)
    earlier = below < across

    def column_of(matrix, i):
        return matrix[:, i : i + 1]

    def count(mask):
        return jnp.sum(jnp.where(mask, 1, 0), axis=0, keepdims=True)

    lines = [turn_a[pl.ds(i, 1), :] for i in range(4)]
    ranks = [
        count((column_of(columns, 0) == lines[0]) & earlier),
        count((column_of(columns, 1) == lines[1]) & earlier) + count(column_of(columns, 0) == lines[1]),
    ]
    places = []
    for i in (2, 3):
        other = column_of(columns, i)
        places.append(count((other > lines[i]) | ((other == lines[i]) & earlier)))
    lane_index = lax.broadcasted_iota(jnp.int32, (1, tokens), 1)
    shift = nz.bit_length() - 1
    for i in range(2):
        turn_b[pl.ds(i, 1), :] = places[i]
    for j in range(2):
        to_ep = experts[j] >> shift
        dx = ((to_ep >> (ny.bit_length() - 1)) - my_x) & (nx - 1)
        dy = ((to_ep & (ny - 1)) - my_y) & (ny - 1)
        hop = jnp.where(long_side[j], turned[j] - 1, jnp.where(turned[j] == 0, GROUPS - 1, nz - 1 - turned[j]))
        line = 2 * hop + jnp.where(long_side[j], 0, 1)
        within = (dx * ny + dy) * MOST + jnp.minimum(ranks[j], MOST - 1)
        list_v[pl.ds(2 + j, 1), :] = jnp.clip(line * (plane * MOST) + within, 0, total * MOST - 1)
        row = jnp.where(long_side[j], places[0], jnp.where(turned[j] == 0, lane_index, places[1]))
        turn_b[pl.ds(2 + j, 1), :] = line * LANES + within
        turn_b[pl.ds(4 + j, 1), :] = row * live
        turn_w[pl.ds(j, 1), :] = route_ref[pl.ds(j, 1), :] * live.astype(F32)
    columns = turn_b[...].T
    weights = turn_w[...].T
    for i in range(2):
        found = jnp.sum(jnp.where(column_of(columns, i) == across, below, 0), axis=0, keepdims=True)
        list_v[pl.ds(i, 1), :] = jnp.clip(found, 0, tokens - 1)
    pick_lists = pltpu.make_async_copy(list_v, list_s, tab_sem.at[0])
    pick_lists.start()
    for i in range(2 * GROUPS):
        hit = [column_of(columns, 2 + j) == across + i * LANES for j in range(2)]
        row = jnp.sum(
            sum(jnp.where(hit[j], column_of(columns, 4 + j), 0) for j in range(2)), axis=0, keepdims=True
        )
        wgt = jnp.sum(
            sum(jnp.where(hit[j], column_of(weights, j), 0.0) for j in range(2)), axis=0, keepdims=True
        )
        limit = CAPS[i % 2][i // 2] if i // 2 < len(CAPS[i % 2]) else tokens
        row_ref[i] = jnp.broadcast_to(jnp.clip(row, 0, limit - 1), (SUB, LANES))
        wgt_ref[i] = jnp.broadcast_to(wgt, (SUB, LANES))
    pick_lists.wait()

    @pl.loop(0, tokens // SUB)
    def _(block):
        for side in range(2):
            picked = [list_s[side, block * SUB + i] for i in range(SUB)]
            rows = [(tok3[token], cot3[token]) for token in picked]
            for i, (a, b) in enumerate(rows):
                own[side, block * SUB + i, 0] = a
                own[side, block * SUB + i, 1] = b

    last_line = 2 * GROUPS - 1
    own_tables = [
        pltpu.make_async_copy(row_ref.at[last_line], row_tab.at[1, GROUPS - 1], tab_sem.at[0]),
        pltpu.make_async_copy(wgt_ref.at[last_line], wgt_tab.at[1, GROUPS - 1], tab_sem.at[1]),
    ]
    for copy in own_tables:
        copy.start()
    pl.semaphore_wait(barrier, 7)
    lanes = [(side, hop) for hop in range(GROUPS) for side in range(2) if hop < len(CAPS[side])]
    for side in range(2):
        hop_copy(side, 0, 0).start()
    meet()
    for side, hop in lanes:
        for copy in table_copies(side, hop):
            copy.start()
    for copy in weight_loads:
        copy.wait()
    weight_copies = [to_partner(0, wg, xg), to_partner(1, wu, xu), to_partner(2, wd, xd)]
    for copy in weight_copies:
        copy.start()
    for side in range(2):
        hop_copy(side, 0, 1).start()
    for copy in own_tables:
        copy.wait()

    def pick(group, side):
        held = None if (group, side) == (GROUPS - 1, 1) else hops[side][group]

        @pl.loop(0, plane)
        def _(cell):
            k = group * per_group + side * plane + cell
            at = [(row_tab[side, group, 0, cell * MOST + r], wgt_tab[side, group, 0, cell * MOST + r]) for r in range(MOST)]
            if held is None:
                rows = [(tok3[row], cot3[row] * wgt) for row, wgt in at]
            else:
                rows = [(held[row, 0], held[row, 1] * wgt) for row, wgt in at]
            for r, (a, b) in enumerate(rows):
                sbuf[k, r] = a
                sbuf[k, MOST + r] = b

    pick(GROUPS - 1, 1)
    send_blocks(GROUPS - 1, 1)

    gh[:, :half], gl[:, :half] = split(wg[...])
    uh[:, :half], ul[:, :half] = split(wu[...])
    dh[:half, :], dl[:half, :] = split(wd[...])
    for ref in (og, ou, od, ag, au, ad):
        ref[...] = jnp.zeros_like(ref)
    for copy in weight_copies:
        copy.wait()
    gh[:, half:], gl[:, half:] = split(xg[...])
    uh[:, half:], ul[:, half:] = split(xu[...])
    dh[half:, :], dl[half:, :] = split(xd[...])
    for side, hop in lanes:
        for copy in table_copies(side, hop):
            copy.wait_recv()
    tables = [
        pltpu.make_async_copy(table.at[side, pl.ds(0, len(CAPS[side]))], to.at[side, pl.ds(0, len(CAPS[side]))], tab_sem.at[i])
        for i, (table, to, side) in enumerate(
            [(row_in, row_tab, 0), (wgt_in, wgt_tab, 0), (row_in, row_tab, 1), (wgt_in, wgt_tab, 1)]
        )
    ]
    for copy in tables:
        copy.start()
    for copy in tables:
        copy.wait()

    flat_in = rbuf.reshape(total * 2 * MOST * SUB, LANES)
    flat_out = tbuf.reshape(total * MOST * SUB, LANES)

    def back(k):
        return remote(tbuf.at[k], bbuf.at[k], back_send_sem, back_recv_sem, behind(k))

    def compute(group):
        first = group * per_group
        block = pl.ds(first, per_group)
        pltpu.make_async_copy(rbuf.at[block], rbuf.at[block], recv_sem.at[group]).wait()
        for r in range(MOST):
            for lane in range(xh.shape[1] // LANES):
                at = (pl.ds(r * per_group, per_group), pl.ds(lane * LANES, LANES))
                start = first * 2 * MOST * SUB + r * SUB + lane
                part = flat_in[pl.ds(start, per_group, stride=2 * MOST * SUB), :]
                xh[at], xl[at] = split(part)
                part = flat_in[pl.ds(start + MOST * SUB, per_group, stride=2 * MOST * SUB), :]
                eh[at], el[at] = split(part)
        x = (xh[...], xl[...])
        e = (eh[...], el[...])
        gate = dot3(x, (gh[...], gl[...]), 1, 0)
        upper = dot3(x, (uh[...], ul[...]), 1, 0)
        d_hidden = dot3(e, (dh[...], dl[...]), 1, 1)
        sig = jax.nn.sigmoid(gate)
        act = gate * sig
        hidden = split(act * upper)
        d_gate = split(d_hidden * upper * sig * (1.0 + gate * (1.0 - sig)))
        d_upper = split(d_hidden * act)
        d_in = dot3(d_gate, (gh[...], gl[...]), 1, 1) + dot3(d_upper, (uh[...], ul[...]), 1, 1)
        for r in range(MOST):
            for lane in range(xh.shape[1] // LANES):
                start = first * MOST * SUB + r * SUB + lane
                flat_out[pl.ds(start, per_group, stride=MOST * SUB), :] = d_in[
                    r * per_group : (r + 1) * per_group, lane * LANES : (lane + 1) * LANES
                ]
        d_gg = dot3(x, d_gate, 0, 0)
        d_uu = dot3(x, d_upper, 0, 0)
        d_dd = dot3(hidden, e, 0, 0)
        ag[...] += d_gg[:, half:]
        au[...] += d_uu[:, half:]
        ad[...] += d_dd[half:, :]
        og[...] += d_gg[:, :half]
        ou[...] += d_uu[:, :half]
        od[...] += d_dd[:half, :]

        own_block = (GROUPS - 1) * per_group + plane

        @pl.loop(0, per_group)
        def _(i):
            k = first + i

            @pl.when(k != own_block)
            def _():
                back(k).start()

            @pl.when(k == own_block)
            def _():
                pltpu.make_async_copy(tbuf.at[own_block], bbuf.at[own_block], back_recv_sem).start()

    @pl.loop(0, GROUPS + 1)
    def _(step):
        for hop in range(GROUPS):

            @pl.when(step == hop)
            def _():
                for side in range(2):
                    if hop < len(CAPS[side]):
                        for part in range(len(hop_parts(side, hop))):
                            hop_copy(side, hop, part).wait_recv()
                            if hop + 1 < len(CAPS[side]) and part < len(hop_parts(side, hop + 1)):
                                hop_copy(side, hop + 1, part).start()
                for side in range(2):
                    if hop < len(CAPS[side]):
                        pick(hop, side)
                for side in range(2):
                    if hop < len(CAPS[side]):
                        send_blocks(hop, side)

        @pl.when(step >= 1)
        def _():
            compute(step - 1)

    grad_copies = [to_partner(3, ag, rg), to_partner(4, au, ru), to_partner(5, ad, rd)]
    for copy in grad_copies:
        copy.start()
    for copy, out, got in zip(grad_copies, (og, ou, od), (rg, ru, rd)):
        copy.wait()
        out[...] += got[...]

    pltpu.make_async_copy(bbuf, bbuf, back_recv_sem).wait()
    stores = [
        pltpu.make_async_copy(src, dst, load_sem.at[i])
        for i, (src, dst) in enumerate([(og, og_ref), (ou, ou_ref), (od, od_ref)])
    ]
    for copy in stores:
        copy.start()

    flat_back = bbuf.reshape(total * MOST, SUB, LANES)

    @pl.loop(0, tokens // SUB)
    def _(block):
        found = []
        for i in range(SUB):
            t = block * SUB + i
            found.append(cot3[t] + (flat_back[list_s[2, t]] + flat_back[list_s[3, t]]))
        for i, value in enumerate(found):
            tok3[block * SUB + i] = value

    for lane in range(SUB):
        gx_ref[:, pl.ds(lane * LANES, LANES)] = flat_tok[pl.ds(lane, tokens, stride=SUB), :]

    for copy in stores:
        copy.wait()
    for side, hop in lanes:
        for part in range(len(hop_parts(side, hop))):
            hop_copy(side, hop, part).wait_send()
        for copy in table_copies(side, hop):
            copy.wait_send()
    sent = pl.ds(0, total - 2 * GROUPS)
    pltpu.make_async_copy(sbuf.at[sent], sbuf.at[sent], send_sem).wait()
    others = pl.ds(0, total - 1)
    pltpu.make_async_copy(tbuf.at[others], tbuf.at[others], back_send_sem).wait()


def settle(*refs):
    ins, outs, held, (load, store) = refs[:4], refs[4:8], refs[8:12], refs[12:]
    loads, stores = [], []
    for i, (src, dst, mid) in enumerate(zip(ins, outs, held)):
        rows = mid.shape[0] // 2
        for part in range(2):
            at = pl.ds(part * rows, rows)
            loads.append(pltpu.make_async_copy(src.at[at], mid.at[at], load.at[i, part]))
            to = dst.at[at] if i == 0 else dst.at[0, at]
            stores.append(pltpu.make_async_copy(mid.at[at], to, store.at[i, part]))
    for copy in loads:
        copy.start()
    for first, second in zip(loads, stores):
        first.wait()
        second.start()
    for copy in stores:
        copy.wait()


def local(nx, ny, nz, tokens, cotangent, w_gate, w_up, w_down, expert_ids, route_weight, halted):
    token_count, width = tokens.shape
    half = w_gate.shape[2]
    plane = nx * ny
    total = nx * ny * nz
    rows = 2 * plane * MOST
    tile = (SUB, LANES)
    vmem = pl.BlockSpec(memory_space=pltpu.VMEM)
    hbm = pl.BlockSpec(memory_space=pl.ANY)
    dma = pltpu.SemaphoreType.DMA
    grad_x, g_gate, g_upper, g_down = pl.pallas_call(
        functools.partial(kernel, nx, ny, nz),
        out_shape=(
            jax.ShapeDtypeStruct((token_count, width), F32),
            jax.ShapeDtypeStruct((width, half), F32),
            jax.ShapeDtypeStruct((width, half), F32),
            jax.ShapeDtypeStruct((half, width), F32),
        ),
        in_specs=[vmem] * 5 + [hbm] * 3,
        out_specs=(vmem,) + (hbm,) * 3,
        scratch_shapes=[
            pltpu.VMEM((width, half), F32),
            pltpu.VMEM((width, half), F32),
            pltpu.VMEM((half, width), F32),
            pltpu.VMEM((width, half), F32),
            pltpu.VMEM((width, half), F32),
            pltpu.VMEM((half, width), F32),
            pltpu.VMEM((token_count,) + tile, F32),
            pltpu.VMEM((token_count,) + tile, F32),
            pltpu.VMEM(tile, jnp.int32),
            pltpu.VMEM(tile, jnp.int32),
            pltpu.VMEM(tile, F32),
            pltpu.VMEM(tile, jnp.int32),
            pltpu.SMEM(tile, jnp.int32),
            pltpu.VMEM((2 * GROUPS,) + tile, jnp.int32),
            pltpu.VMEM((2 * GROUPS,) + tile, F32),
            pltpu.VMEM((2, token_count, 2) + tile, F32),
            tuple(tuple(pltpu.VMEM((cap, 2) + tile, F32) for cap in caps) for caps in CAPS),
            pltpu.VMEM((2, GROUPS) + tile, jnp.int32),
            pltpu.VMEM((2, GROUPS) + tile, F32),
            pltpu.SMEM((2, GROUPS) + tile, jnp.int32),
            pltpu.SMEM((2, GROUPS) + tile, F32),
            pltpu.VMEM((total, 2 * MOST) + tile, F32),
            pltpu.VMEM((total, 2 * MOST) + tile, F32),
            pltpu.VMEM((total, MOST) + tile, F32),
            pltpu.VMEM((total, MOST) + tile, F32),
            pltpu.VMEM((width, half), F32),
            pltpu.VMEM((width, half), F32),
            pltpu.VMEM((half, width), F32),
            pltpu.VMEM((width, 2 * half), BF16),
            pltpu.VMEM((width, 2 * half), BF16),
            pltpu.VMEM((width, 2 * half), BF16),
            pltpu.VMEM((width, 2 * half), BF16),
            pltpu.VMEM((2 * half, width), BF16),
            pltpu.VMEM((2 * half, width), BF16),
            pltpu.VMEM((width, half), F32),
            pltpu.VMEM((width, half), F32),
            pltpu.VMEM((half, width), F32),
            pltpu.VMEM((width, half), F32),
            pltpu.VMEM((width, half), F32),
            pltpu.VMEM((half, width), F32),
            pltpu.VMEM((rows, width), BF16),
            pltpu.VMEM((rows, width), BF16),
            pltpu.VMEM((rows, width), BF16),
            pltpu.VMEM((rows, width), BF16),
            dma((3,)),
            pltpu.SemaphoreType.REGULAR((nz // 2 - 1 + nx // 2 + ny // 2,)),
            dma((2, GROUPS, 2)),
            dma((2, GROUPS, 2)),
            dma((2 * GROUPS,)),
            dma((2, GROUPS)),
            dma((2 * GROUPS,)),
            dma((2, GROUPS)),
            dma((4,)),
            dma,
            dma((GROUPS,)),
            dma,
            dma,
            dma((6,)),
            dma((6,)),
        ],
        compiler_params=pltpu.CompilerParams(
            collective_id=0, has_side_effects=True, vmem_limit_bytes=63 * 1024 * 1024
        ),
    )(
        expert_ids.T,
        route_weight.T,
        halted.reshape(1, token_count),
        tokens,
        cotangent,
        w_gate[0],
        w_up[0],
        w_down[0],
    )
    arrays = (grad_x, g_gate, g_upper, g_down)
    return pl.pallas_call(
        settle,
        out_shape=(jax.ShapeDtypeStruct(grad_x.shape, F32),)
        + tuple(jax.ShapeDtypeStruct((1,) + array.shape, F32) for array in arrays[1:]),
        in_specs=[hbm] * 4,
        out_specs=(hbm,) * 4,
        scratch_shapes=[pltpu.VMEM(array.shape, F32) for array in arrays] + [dma((4, 2)), dma((4, 2))],
    )(*arrays)


def solution(mesh):
    nx, ny = 4, 4
    nz = mesh.shape["dp"] // 2
    spec2 = P(("ep", "dp"), None)
    spec3 = P(("ep", "dp"), None, None)
    return jax.shard_map(
        functools.partial(local, nx, ny, nz),
        mesh=mesh,
        in_specs=(spec2, spec2, spec3, spec3, spec3, spec2, spec2, P(("ep", "dp"))),
        out_specs=(spec2, spec3, spec3, spec3),
        check_vma=False,
    )
```

```python
import functools

import jax
import jax.numpy as jnp
from jax import lax
from jax.experimental import pallas as pl
from jax.experimental.pallas import tpu as pltpu
from jax.sharding import PartitionSpec as P

MESH = pl.DeviceIdType.MESH
MOST = 3
GROUPS = 4
FIRST = 48
BOUNDS = ((128, 128, 96, 48), (128, 96, 48))
USUAL = ((112, 96, 80, 48), (96, 80, 48))
LANES = 128
SUB = 8
F32 = jnp.float32
BF16 = jnp.bfloat16


def split(value):
    high = value.astype(BF16)
    return high, (value - high.astype(F32)).astype(BF16)


def dot3(a, b, a_dim, b_dim):
    def dot(p, q):
        return lax.dot_general(p, q, (((a_dim,), (b_dim,)), ((), ())), preferred_element_type=F32)

    return dot(a[0], b[0]) + dot(a[0], b[1]) + dot(a[1], b[0])


def kernel(
    caps,
    nx,
    ny,
    nz,
    ids_ref,
    route_ref,
    halt_ref,
    tok_ref,
    cot_ref,
    wg_ref,
    wu_ref,
    wd_ref,
    gx_ref,
    og_ref,
    ou_ref,
    od_ref,
    flag_ref,
    wg,
    wu,
    wd,
    og,
    ou,
    od,
    tok3,
    cot3,
    turn_a,
    turn_b,
    turn_w,
    list_v,
    list_s,
    flag_in,
    flag_out,
    flag_pair,
    row_ref,
    wgt_ref,
    own,
    hops,
    row_in,
    wgt_in,
    row_tab,
    wgt_tab,
    sbuf,
    rbuf,
    tbuf,
    bbuf,
    xg,
    xu,
    xd,
    gh,
    gl,
    uh,
    ul,
    dh,
    dl,
    ag,
    au,
    ad,
    rg,
    ru,
    rd,
    xh,
    xl,
    eh,
    el,
    load_sem,
    meet_sem,
    hop_send_sem,
    hop_recv_sem,
    row_send_sem,
    row_recv_sem,
    wgt_send_sem,
    wgt_recv_sem,
    tab_sem,
    send_sem,
    recv_sem,
    back_send_sem,
    back_recv_sem,
    flag_send_sem,
    flag_recv_sem,
    pair_send_sem,
    pair_recv_sem,
):
    ep = lax.axis_index("ep")
    dp = lax.axis_index("dp")
    my_x, my_y = ep // ny, ep % ny
    my_z, my_c = dp // 2, dp % 2
    sign = 1 - 2 * my_c
    plane = nx * ny
    per_group = 2 * plane
    total = nz * plane
    half = wg.shape[1]
    tokens, width = tok_ref.shape
    low_bits = nz - 1
    partner = (ep, my_z * 2 + 1 - my_c)

    def column(step):
        return ep, ((my_z + nz + step) % nz) * 2 + my_c

    def offset(k):
        group, low = k // per_group, k % per_group
        side, cell = low // plane, low % plane
        hop = group + 1
        dz = jnp.where(side == 0, sign * hop, jnp.where(group == GROUPS - 1, 0, -sign * hop))
        return cell // ny, cell % ny, dz

    def behind(k):
        dx, dy, dz = offset(k)
        return ((my_x + nx - dx) % nx) * ny + (my_y + ny - dy) % ny, ((my_z + nz - dz) % nz) * 2 + my_c

    def beside(cell):
        return ((my_x + cell // ny) % nx) * ny + (my_y + cell % ny) % ny, dp

    barrier = pltpu.get_barrier_semaphore()

    def at_xy(dx, dy):
        return ((my_x + nx + dx) % nx) * ny + (my_y + ny + dy) % ny, dp

    rings = (
        (column(1), column(-1)),
        (at_xy(1, 0), at_xy(-1, 0)),
        (at_xy(0, 1), at_xy(0, -1)),
    )
    for device in [device for ring in rings for device in ring] + [partner]:
        pl.semaphore_signal(barrier, inc=1, device_id=device, device_id_type=MESH)

    weight_loads = [
        pltpu.make_async_copy(src, dst, load_sem.at[i])
        for i, (src, dst) in enumerate([(wg_ref, wg), (wu_ref, wu), (wd_ref, wd)])
    ]
    for copy in weight_loads:
        copy.start()

    def meet():
        turn = 0
        for ring, length in zip(rings, (nz, nx, ny)):
            for _ in range(length // 2 - (1 if length == nz else 0)):
                for device in ring:
                    pl.semaphore_signal(meet_sem.at[turn], inc=1, device_id=device, device_id_type=MESH)
                pl.semaphore_wait(meet_sem.at[turn], 2)
                turn += 1

    def remote(src, dst, send, recv, device):
        return pltpu.make_async_remote_copy(
            src_ref=src, dst_ref=dst, send_sem=send, recv_sem=recv, device_id=device, device_id_type=MESH
        )

    def toward(side):
        return column(sign if side == 0 else -sign)

    def hop_parts(side, hop):
        cap = caps[side][hop]
        return ((0, FIRST), (FIRST, cap)) if cap > FIRST else ((0, cap),)

    def hop_copy(side, hop, part):
        start, end = hop_parts(side, hop)[part]
        rows = pl.ds(start, end - start)
        src = own.at[side, rows] if hop == 0 else hops[side][hop - 1].at[rows]
        return remote(
            src,
            hops[side][hop].at[rows],
            hop_send_sem.at[side, hop, part],
            hop_recv_sem.at[side, hop, part],
            toward(side),
        )

    def table_copies(side, hop):
        device = column(sign * (hop + 1) if side == 0 else -sign * (hop + 1))
        at = 2 * hop + side
        return (
            remote(row_ref.at[at], row_in.at[side, hop], row_send_sem.at[at], row_recv_sem.at[side, hop], device),
            remote(wgt_ref.at[at], wgt_in.at[side, hop], wgt_send_sem.at[at], wgt_recv_sem.at[side, hop], device),
        )

    def block_copy(k, group, cell):
        return remote(sbuf.at[k], rbuf.at[k], send_sem, recv_sem.at[group], beside(cell))

    def send_blocks(group, side):
        first = group * per_group + side * plane
        pltpu.make_async_copy(sbuf.at[first], rbuf.at[first], recv_sem.at[group]).start()

        @pl.loop(1, plane)
        def _(cell):
            block_copy(first + cell, group, cell).start()

    def to_partner(i, src, dst):
        return remote(src, dst, pair_send_sem.at[i], pair_recv_sem.at[i], partner)

    flat_tok = tok3.reshape(tokens * SUB, LANES)
    flat_cot = cot3.reshape(tokens * SUB, LANES)
    for lane in range(SUB):
        at = pl.ds(lane * LANES, LANES)
        to = pl.ds(lane, tokens, stride=SUB)
        flat_tok[to, :] = tok_ref[:, at]
        flat_cot[to, :] = cot_ref[:, at]

    live = 1 - halt_ref[...]
    experts = [ids_ref[pl.ds(j, 1), :] for j in range(2)]
    turned = [(sign * ((e & low_bits) - my_z)) & low_bits for e in experts]
    long_side = [(t >= 1) & (t <= GROUPS) for t in turned]
    short_side = [t > GROUPS for t in turned]
    far = [
        jnp.maximum(*[jnp.where(m, t, 0) for m, t in zip(long_side, turned)]) * live,
        jnp.maximum(*[jnp.where(m, nz - t, 0) for m, t in zip(short_side, turned)]) * live,
    ]
    for ref in (turn_a, turn_b, turn_w):
        ref[...] = jnp.zeros_like(ref)
    list_v[...] = jnp.zeros_like(list_v)
    for i, line in enumerate(experts + far):
        turn_a[pl.ds(i, 1), :] = line
    columns = turn_a[...].T
    below = lax.broadcasted_iota(jnp.int32, (tokens, tokens), 0)
    across = lax.broadcasted_iota(jnp.int32, (tokens, tokens), 1)
    earlier = below < across

    def column_of(matrix, i):
        return matrix[:, i : i + 1]

    def count(mask):
        return jnp.sum(jnp.where(mask, 1, 0), axis=0, keepdims=True)

    lines = [turn_a[pl.ds(i, 1), :] for i in range(4)]
    ranks = [
        count((column_of(columns, 0) == lines[0]) & earlier),
        count((column_of(columns, 1) == lines[1]) & earlier) + count(column_of(columns, 0) == lines[1]),
    ]
    places = []
    for i in (2, 3):
        other = column_of(columns, i)
        places.append(count((other > lines[i]) | ((other == lines[i]) & earlier)))
    lane_index = lax.broadcasted_iota(jnp.int32, (1, tokens), 1)
    over = jnp.zeros((1, 1), jnp.int32)
    for side in range(2):
        for hop, cap in enumerate(caps[side]):
            needed = jnp.sum(jnp.where(far[side] > hop, 1, 0), axis=1, keepdims=True)
            over += jnp.where(needed > cap, 1, 0)
    flag_lane = lane_index == LANES - 1
    shift = nz.bit_length() - 1
    for i in range(2):
        turn_b[pl.ds(i, 1), :] = places[i]
    for j in range(2):
        to_ep = experts[j] >> shift
        dx = ((to_ep >> (ny.bit_length() - 1)) - my_x) & (nx - 1)
        dy = ((to_ep & (ny - 1)) - my_y) & (ny - 1)
        hop = jnp.where(long_side[j], turned[j] - 1, jnp.where(turned[j] == 0, GROUPS - 1, nz - 1 - turned[j]))
        line = 2 * hop + jnp.where(long_side[j], 0, 1)
        within = (dx * ny + dy) * MOST + jnp.minimum(ranks[j], MOST - 1)
        list_v[pl.ds(2 + j, 1), :] = jnp.clip(line * (plane * MOST) + within, 0, total * MOST - 1)
        row = jnp.where(long_side[j], places[0], jnp.where(turned[j] == 0, lane_index, places[1]))
        turn_b[pl.ds(2 + j, 1), :] = line * LANES + within
        turn_b[pl.ds(4 + j, 1), :] = row * live
        turn_w[pl.ds(j, 1), :] = route_ref[pl.ds(j, 1), :] * live.astype(F32)
    columns = turn_b[...].T
    weights = turn_w[...].T
    for i in range(2):
        found = jnp.sum(jnp.where(column_of(columns, i) == across, below, 0), axis=0, keepdims=True)
        list_v[pl.ds(i, 1), :] = jnp.clip(found, 0, tokens - 1)
    pick_lists = pltpu.make_async_copy(list_v, list_s, tab_sem.at[0])
    pick_lists.start()
    for i in range(2 * GROUPS):
        hit = [column_of(columns, 2 + j) == across + i * LANES for j in range(2)]
        row = jnp.sum(
            sum(jnp.where(hit[j], column_of(columns, 4 + j), 0) for j in range(2)), axis=0, keepdims=True
        )
        wgt = jnp.sum(
            sum(jnp.where(hit[j], column_of(weights, j), 0.0) for j in range(2)), axis=0, keepdims=True
        )
        limit = caps[i % 2][i // 2] if i // 2 < len(caps[i % 2]) else tokens
        row_ref[i] = jnp.broadcast_to(jnp.clip(row, 0, limit - 1), (SUB, LANES))
        wgt_ref[i] = jnp.broadcast_to(jnp.where(flag_lane, over.astype(F32), wgt), (SUB, LANES))
    pick_lists.wait()

    @pl.loop(0, tokens // SUB)
    def _(block):
        for side in range(2):
            picked = [list_s[side, block * SUB + i] for i in range(SUB)]
            rows = [(tok3[token], cot3[token]) for token in picked]
            for i, (a, b) in enumerate(rows):
                own[side, block * SUB + i, 0] = a
                own[side, block * SUB + i, 1] = b

    last_line = 2 * GROUPS - 1
    own_tables = [
        pltpu.make_async_copy(row_ref.at[last_line], row_tab.at[1, GROUPS - 1], tab_sem.at[0]),
        pltpu.make_async_copy(wgt_ref.at[last_line], wgt_tab.at[1, GROUPS - 1], tab_sem.at[1]),
    ]
    for copy in own_tables:
        copy.start()
    pl.semaphore_wait(barrier, 7)
    lanes = [(side, hop) for hop in range(GROUPS) for side in range(2) if hop < len(caps[side])]
    for side in range(2):
        hop_copy(side, 0, 0).start()
    meet()
    for side, hop in lanes:
        for copy in table_copies(side, hop):
            copy.start()
    for copy in weight_loads:
        copy.wait()
    weight_copies = [to_partner(0, wg, xg), to_partner(1, wu, xu), to_partner(2, wd, xd)]
    for copy in weight_copies:
        copy.start()
    for side in range(2):
        hop_copy(side, 0, 1).start()
    for copy in own_tables:
        copy.wait()

    def pick(group, side):
        held = None if (group, side) == (GROUPS - 1, 1) else hops[side][group]

        @pl.loop(0, plane)
        def _(cell):
            k = group * per_group + side * plane + cell
            at = [(row_tab[side, group, 0, cell * MOST + r], wgt_tab[side, group, 0, cell * MOST + r]) for r in range(MOST)]
            if held is None:
                rows = [(tok3[row], cot3[row] * wgt) for row, wgt in at]
            else:
                rows = [(held[row, 0], held[row, 1] * wgt) for row, wgt in at]
            for r, (a, b) in enumerate(rows):
                sbuf[k, r] = a
                sbuf[k, MOST + r] = b

    pick(GROUPS - 1, 1)
    send_blocks(GROUPS - 1, 1)

    gh[:, :half], gl[:, :half] = split(wg[...])
    uh[:, :half], ul[:, :half] = split(wu[...])
    dh[:half, :], dl[:half, :] = split(wd[...])
    for ref in (og, ou, od, ag, au, ad):
        ref[...] = jnp.zeros_like(ref)
    for copy in weight_copies:
        copy.wait()
    gh[:, half:], gl[:, half:] = split(xg[...])
    uh[:, half:], ul[:, half:] = split(xu[...])
    dh[half:, :], dl[half:, :] = split(xd[...])
    for side, hop in lanes:
        for copy in table_copies(side, hop):
            copy.wait_recv()
    tables = [
        pltpu.make_async_copy(table.at[side, pl.ds(0, len(caps[side]))], to.at[side, pl.ds(0, len(caps[side]))], tab_sem.at[i])
        for i, (table, to, side) in enumerate(
            [(row_in, row_tab, 0), (wgt_in, wgt_tab, 0), (row_in, row_tab, 1), (wgt_in, wgt_tab, 1)]
        )
    ]
    for copy in tables:
        copy.start()
    for copy in tables:
        copy.wait()

    in_column = wgt_ref[0]
    for side, hop in lanes:
        in_column += wgt_in[side, hop]
    flag_out[0] = in_column

    def flag_copy(cell):
        return remote(flag_out.at[0], flag_in.at[cell], flag_send_sem, flag_recv_sem, beside(cell))

    flat_in = rbuf.reshape(total * 2 * MOST * SUB, LANES)
    flat_out = tbuf.reshape(total * MOST * SUB, LANES)

    def back(k):
        return remote(tbuf.at[k], bbuf.at[k], back_send_sem, back_recv_sem, behind(k))

    def compute(group):
        first = group * per_group
        block = pl.ds(first, per_group)
        pltpu.make_async_copy(rbuf.at[block], rbuf.at[block], recv_sem.at[group]).wait()
        for r in range(MOST):
            for lane in range(xh.shape[1] // LANES):
                at = (pl.ds(r * per_group, per_group), pl.ds(lane * LANES, LANES))
                start = first * 2 * MOST * SUB + r * SUB + lane
                part = flat_in[pl.ds(start, per_group, stride=2 * MOST * SUB), :]
                xh[at], xl[at] = split(part)
                part = flat_in[pl.ds(start + MOST * SUB, per_group, stride=2 * MOST * SUB), :]
                eh[at], el[at] = split(part)
        x = (xh[...], xl[...])
        e = (eh[...], el[...])
        gate = dot3(x, (gh[...], gl[...]), 1, 0)
        upper = dot3(x, (uh[...], ul[...]), 1, 0)
        d_hidden = dot3(e, (dh[...], dl[...]), 1, 1)
        sig = jax.nn.sigmoid(gate)
        act = gate * sig
        hidden = split(act * upper)
        d_gate = split(d_hidden * upper * sig * (1.0 + gate * (1.0 - sig)))
        d_upper = split(d_hidden * act)
        d_in = dot3(d_gate, (gh[...], gl[...]), 1, 1) + dot3(d_upper, (uh[...], ul[...]), 1, 1)
        for r in range(MOST):
            for lane in range(xh.shape[1] // LANES):
                start = first * MOST * SUB + r * SUB + lane
                flat_out[pl.ds(start, per_group, stride=MOST * SUB), :] = d_in[
                    r * per_group : (r + 1) * per_group, lane * LANES : (lane + 1) * LANES
                ]
        d_gg = dot3(x, d_gate, 0, 0)
        d_uu = dot3(x, d_upper, 0, 0)
        d_dd = dot3(hidden, e, 0, 0)
        ag[...] += d_gg[:, half:]
        au[...] += d_uu[:, half:]
        ad[...] += d_dd[half:, :]
        og[...] += d_gg[:, :half]
        ou[...] += d_uu[:, :half]
        od[...] += d_dd[:half, :]

        own_block = (GROUPS - 1) * per_group + plane

        @pl.loop(0, per_group)
        def _(i):
            k = first + i

            @pl.when(k != own_block)
            def _():
                back(k).start()

            @pl.when(k == own_block)
            def _():
                pltpu.make_async_copy(tbuf.at[own_block], bbuf.at[own_block], back_recv_sem).start()

    @pl.loop(1, plane)
    def _(cell):
        flag_copy(cell).start()

    @pl.loop(0, GROUPS + 1)
    def _(step):
        for hop in range(GROUPS):

            @pl.when(step == hop)
            def _():
                for side in range(2):
                    if hop < len(caps[side]):
                        for part in range(len(hop_parts(side, hop))):
                            hop_copy(side, hop, part).wait_recv()
                            if hop + 1 < len(caps[side]) and part < len(hop_parts(side, hop + 1)):
                                hop_copy(side, hop + 1, part).start()
                for side in range(2):
                    if hop < len(caps[side]):
                        pick(hop, side)
                for side in range(2):
                    if hop < len(caps[side]):
                        send_blocks(hop, side)

        @pl.when(step >= 1)
        def _():
            compute(step - 1)

    other_flags = flag_in.at[pl.ds(1, plane - 1)]
    pltpu.make_async_copy(other_flags, other_flags, flag_recv_sem).wait()
    pltpu.make_async_copy(other_flags, other_flags, flag_send_sem).wait()
    in_core = flag_out[0]
    for cell in range(1, plane):
        in_core += flag_in[cell]
    flag_out[1] = in_core
    grad_copies = [to_partner(3, ag, rg), to_partner(4, au, ru), to_partner(5, ad, rd)]
    for copy in grad_copies:
        copy.start()
    for copy, out, got in zip(grad_copies, (og, ou, od), (rg, ru, rd)):
        copy.wait()
        out[...] += got[...]

    flag_swap = to_partner(6, flag_out.at[1], flag_pair)
    flag_swap.start()
    pltpu.make_async_copy(bbuf, bbuf, back_recv_sem).wait()
    flag_swap.wait()
    flag_ref[...] = flag_out[1] + flag_pair[...]
    stores = [
        pltpu.make_async_copy(src, dst, load_sem.at[i])
        for i, (src, dst) in enumerate([(og, og_ref), (ou, ou_ref), (od, od_ref)])
    ]
    for copy in stores:
        copy.start()

    flat_back = bbuf.reshape(total * MOST, SUB, LANES)

    @pl.loop(0, tokens // SUB)
    def _(block):
        found = []
        for i in range(SUB):
            t = block * SUB + i
            found.append(cot3[t] + (flat_back[list_s[2, t]] + flat_back[list_s[3, t]]))
        for i, value in enumerate(found):
            tok3[block * SUB + i] = value

    for lane in range(SUB):
        gx_ref[:, pl.ds(lane * LANES, LANES)] = flat_tok[pl.ds(lane, tokens, stride=SUB), :]

    for copy in stores:
        copy.wait()
    for side, hop in lanes:
        for part in range(len(hop_parts(side, hop))):
            hop_copy(side, hop, part).wait_send()
        for copy in table_copies(side, hop):
            copy.wait_send()
    sent = pl.ds(0, total - 2 * GROUPS)
    pltpu.make_async_copy(sbuf.at[sent], sbuf.at[sent], send_sem).wait()
    others = pl.ds(0, total - 1)
    pltpu.make_async_copy(tbuf.at[others], tbuf.at[others], back_send_sem).wait()


def settle(*refs):
    ins, outs, held, (load, store) = refs[:4], refs[4:8], refs[8:12], refs[12:]
    loads, stores = [], []
    for i, (src, dst, mid) in enumerate(zip(ins, outs, held)):
        rows = mid.shape[0] // 2
        for part in range(2):
            at = pl.ds(part * rows, rows)
            loads.append(pltpu.make_async_copy(src.at[at], mid.at[at], load.at[i, part]))
            to = dst.at[at] if i == 0 else dst.at[0, at]
            stores.append(pltpu.make_async_copy(mid.at[at], to, store.at[i, part]))
    for copy in loads:
        copy.start()
    for first, second in zip(loads, stores):
        first.wait()
        second.start()
    for copy in stores:
        copy.wait()


def local(nx, ny, nz, tokens, cotangent, w_gate, w_up, w_down, expert_ids, route_weight, halted):
    token_count, width = tokens.shape
    half = w_gate.shape[2]
    plane = nx * ny
    total = nx * ny * nz
    rows = 2 * plane * MOST
    tile = (SUB, LANES)
    vmem = pl.BlockSpec(memory_space=pltpu.VMEM)
    hbm = pl.BlockSpec(memory_space=pl.ANY)
    dma = pltpu.SemaphoreType.DMA
    def layer(caps, number):
        return pl.pallas_call(
            functools.partial(kernel, caps, nx, ny, nz),
            out_shape=(
                jax.ShapeDtypeStruct((token_count, width), F32),
                jax.ShapeDtypeStruct((width, half), F32),
                jax.ShapeDtypeStruct((width, half), F32),
                jax.ShapeDtypeStruct((half, width), F32),
                jax.ShapeDtypeStruct(tile, F32),
            ),
            in_specs=[vmem] * 5 + [hbm] * 3,
            out_specs=(vmem,) + (hbm,) * 3 + (vmem,),
            scratch_shapes=[
                pltpu.VMEM((width, half), F32),
                pltpu.VMEM((width, half), F32),
                pltpu.VMEM((half, width), F32),
                pltpu.VMEM((width, half), F32),
                pltpu.VMEM((width, half), F32),
                pltpu.VMEM((half, width), F32),
                pltpu.VMEM((token_count,) + tile, F32),
                pltpu.VMEM((token_count,) + tile, F32),
                pltpu.VMEM(tile, jnp.int32),
                pltpu.VMEM(tile, jnp.int32),
                pltpu.VMEM(tile, F32),
                pltpu.VMEM(tile, jnp.int32),
                pltpu.SMEM(tile, jnp.int32),
                pltpu.VMEM((plane,) + tile, F32),
                pltpu.VMEM((2,) + tile, F32),
                pltpu.VMEM(tile, F32),
                pltpu.VMEM((2 * GROUPS,) + tile, jnp.int32),
                pltpu.VMEM((2 * GROUPS,) + tile, F32),
                pltpu.VMEM((2, token_count, 2) + tile, F32),
                tuple(tuple(pltpu.VMEM((cap, 2) + tile, F32) for cap in side) for side in caps),
                pltpu.VMEM((2, GROUPS) + tile, jnp.int32),
                pltpu.VMEM((2, GROUPS) + tile, F32),
                pltpu.SMEM((2, GROUPS) + tile, jnp.int32),
                pltpu.SMEM((2, GROUPS) + tile, F32),
                pltpu.VMEM((total, 2 * MOST) + tile, F32),
                pltpu.VMEM((total, 2 * MOST) + tile, F32),
                pltpu.VMEM((total, MOST) + tile, F32),
                pltpu.VMEM((total, MOST) + tile, F32),
                pltpu.VMEM((width, half), F32),
                pltpu.VMEM((width, half), F32),
                pltpu.VMEM((half, width), F32),
                pltpu.VMEM((width, 2 * half), BF16),
                pltpu.VMEM((width, 2 * half), BF16),
                pltpu.VMEM((width, 2 * half), BF16),
                pltpu.VMEM((width, 2 * half), BF16),
                pltpu.VMEM((2 * half, width), BF16),
                pltpu.VMEM((2 * half, width), BF16),
                pltpu.VMEM((width, half), F32),
                pltpu.VMEM((width, half), F32),
                pltpu.VMEM((half, width), F32),
                pltpu.VMEM((width, half), F32),
                pltpu.VMEM((width, half), F32),
                pltpu.VMEM((half, width), F32),
                pltpu.VMEM((rows, width), BF16),
                pltpu.VMEM((rows, width), BF16),
                pltpu.VMEM((rows, width), BF16),
                pltpu.VMEM((rows, width), BF16),
                dma((3,)),
                pltpu.SemaphoreType.REGULAR((nz // 2 - 1 + nx // 2 + ny // 2,)),
                dma((2, GROUPS, 2)),
                dma((2, GROUPS, 2)),
                dma((2 * GROUPS,)),
                dma((2, GROUPS)),
                dma((2 * GROUPS,)),
                dma((2, GROUPS)),
                dma((4,)),
                dma,
                dma((GROUPS,)),
                dma,
                dma,
                dma,
                dma,
                dma((7,)),
                dma((7,)),
            ],
            compiler_params=pltpu.CompilerParams(
                collective_id=number, has_side_effects=True, vmem_limit_bytes=63 * 1024 * 1024
            ),
        )(
            expert_ids.T,
            route_weight.T,
            halted.reshape(1, token_count),
            tokens,
            cotangent,
            w_gate[0],
            w_up[0],
            w_down[0],
        )

    def settled(arrays):
        return pl.pallas_call(
            settle,
            out_shape=(jax.ShapeDtypeStruct(arrays[0].shape, F32),)
            + tuple(jax.ShapeDtypeStruct((1,) + array.shape, F32) for array in arrays[1:]),
            in_specs=[hbm] * 4,
            out_specs=(hbm,) * 4,
            scratch_shapes=[pltpu.VMEM(array.shape, F32) for array in arrays] + [dma((4, 2)), dma((4, 2))],
        )(*arrays)

    *arrays, flag = layer(USUAL, 0)
    return lax.cond(
        flag[0, LANES - 1] > 0.0,
        lambda _: settled(layer(BOUNDS, 1)[:4]),
        settled,
        tuple(arrays),
    )


def solution(mesh):
    nx, ny = 4, 4
    nz = mesh.shape["dp"] // 2
    spec2 = P(("ep", "dp"), None)
    spec3 = P(("ep", "dp"), None, None)
    return jax.shard_map(
        functools.partial(local, nx, ny, nz),
        mesh=mesh,
        in_specs=(spec2, spec2, spec3, spec3, spec3, spec2, spec2, P(("ep", "dp"))),
        out_specs=(spec2, spec3, spec3, spec3),
        check_vma=False,
    )
```
